32 devices in a mesh: row: 4 (over x, core), col: 8 (over z, y).
Axes of the slice: x: 2, y: 2, z: 4, core: 2. Of those that a mesh axis runs over, the one named last changes fastest.
Arguments:
- node_features: bfloat16 [4096, 256], P(('row', 'col')), may hold values from -6 to 6
- layer_weight: bfloat16 [256, 256], replicated, may hold values from -0.375 to 0.375
- output_grad: bfloat16 [4096, 256], P(('row', 'col')), may hold values from -6 to 6
- block_values: bfloat16 [4, 8, 24, 128, 128], P('row', 'col'), may hold values from -0.15625 to 0.15625
- block_position: int32 [4, 8, 24], P('row', 'col'), may hold values from 0 to 31, as said below
- tile_count: int32 [4, 8], P('row', 'col'), may hold values from 6 to 24, as said below
Outputs:
- node_output: bfloat16 [4096, 256], P(('row', 'col'))
- input_grad: bfloat16 [4096, 256], P(('row', 'col'))
- weight_grad: float32 [256, 256], replicated
The draws below stay inside these ranges and needn't reach their ends.
Inputs may be any that keep to these rules, and one draw needn't show every extreme that they name: Tile (r, c) uses its slots 0 to tile_count[r, c] - 1; in every draw some tile uses all 24 slots. `block_position`: the slots of a tile hold distinct positions in increasing order.
All inputs are finite; a program needn't handle non-finite values.
Results may differ from the reference program's by a relative error of at most 0.02.
Values may be sent and summed in bfloat16 or wider, within the bound.
A program may use at most 64 MiB of HBM per device.

```python
import math
import jax
import jax.numpy as jnp
from jax import lax

WIDTH = 256
BLOCK = 128
NODE_DEV = 128
GRID_ROWS = 4
GRID_COLS = 8
ROW_PANEL = 1024
COL_PANEL = 512
ROW_BLOCKS = 8
COL_BLOCKS = 4
SLOTS = 24
NODES = 4096


def draw_block_position(key, part):
    tile_keys = jax.random.split(jax.random.fold_in(key, 7), GRID_ROWS * GRID_COLS)

    def one_tile(tile_key):
        shuffled = jax.random.permutation(tile_key, ROW_BLOCKS * COL_BLOCKS)
        return jnp.sort(shuffled[:SLOTS])
    chosen = jax.vmap(one_tile)(tile_keys)
    return chosen.reshape(GRID_ROWS, GRID_COLS, SLOTS).astype(jnp.int32)


def draw_tile_count(key, part):
    first_key = jax.random.fold_in(key, 11)
    second_key = jax.random.fold_in(key, 12)
    third_key = jax.random.fold_in(key, 13)
    base_count = jax.random.randint(first_key, (GRID_ROWS, GRID_COLS), SLOTS // 4, SLOTS // 2 + 1)
    heavy_tile = jax.random.randint(second_key, (GRID_ROWS, GRID_COLS), 0, 8) == 0
    counts = jnp.where(heavy_tile, SLOTS, base_count).reshape(-1)
    chosen_tile = jax.random.randint(third_key, (), 0, GRID_ROWS * GRID_COLS)
    counts = counts.at[chosen_tile].set(SLOTS)
    return counts.reshape(GRID_ROWS, GRID_COLS).astype(jnp.int32)


def block_levels(key, extent, cuts, low, high):
    def one(dim, blocks):
        heights = jax.random.uniform(jax.random.fold_in(jax.random.fold_in(key, 6), dim), (blocks,), jnp.float32, low / len(cuts), high / len(cuts))
        return jnp.repeat(jnp.exp(heights), extent[dim] // blocks).reshape((-1,) + (1,) * (len(extent) - dim - 1))

    factor_of = one(*cuts[0])
    for cut in cuts[1:]:
        factor_of = factor_of * one(*cut)
    return factor_of


def scatter_about(own_key, extent, deviation, reach, shards=(), kind=jnp.bfloat16):
    level = block_levels(own_key, extent, shards, -0.22, 0.18) if shards else 1.0
    array = jax.random.normal(own_key, extent, jnp.float32) * deviation * level
    return jnp.minimum(jnp.maximum(array, -reach), reach).astype(kind)


def setup_inputs(seed: int = 0) -> dict:
    streams_of = jax.random.split(jax.random.key(seed), 7)
    node_features = scatter_about(streams_of[0], (NODES, WIDTH), 1.0, 6.0, ((0, 32),))
    layer_weight = scatter_about(streams_of[1], (WIDTH, WIDTH), WIDTH ** -0.5, 0.375)
    output_grad = scatter_about(streams_of[2], (NODES, WIDTH), 1.0, 6.0, ((0, 32),))
    block_values = scatter_about(streams_of[3], (GRID_ROWS, GRID_COLS, SLOTS, BLOCK, BLOCK), (SLOTS * BLOCK * BLOCK // (2 * NODE_DEV)) ** -0.5, 0.15625, ((0, 4), (1, 8)))
    block_position = draw_block_position(jax.random.fold_in(streams_of[6], 71), 0)
    tile_count = draw_tile_count(jax.random.fold_in(streams_of[6], 71), 0)
    return dict(node_features=node_features, layer_weight=layer_weight, output_grad=output_grad, block_values=block_values, block_position=block_position, tile_count=tile_count)


def elu_slope(pre_activation):
    return jnp.where(pre_activation > 0, 1.0, jnp.exp(jnp.minimum(pre_activation, 0.0)))

def rounded(partial_value):
    return lax.optimization_barrier(partial_value.astype(jnp.bfloat16)).astype(jnp.float32)

def forward_tile(values, position, count, panel_rows):
    block_row = position // COL_BLOCKS
    block_col = position % COL_BLOCKS
    live = (jnp.arange(SLOTS, dtype=jnp.int32) < count).astype(jnp.float32)
    picked = panel_rows.reshape(COL_BLOCKS, BLOCK, WIDTH)[block_col]
    product = jnp.einsum('nij,njf->nif', values.astype(jnp.float32), picked.astype(jnp.float32))
    product = product * live[:, None, None]
    summed = jax.ops.segment_sum(product, block_row, num_segments=ROW_BLOCKS)
    return summed.reshape(ROW_PANEL, WIDTH)

def backward_tile(values, position, count, panel_rows):
    block_row = position // COL_BLOCKS
    block_col = position % COL_BLOCKS
    live = (jnp.arange(SLOTS, dtype=jnp.int32) < count).astype(jnp.float32)
    picked = panel_rows.reshape(ROW_BLOCKS, BLOCK, WIDTH)[block_row]
    product = jnp.einsum('nij,nif->njf', values.astype(jnp.float32), picked.astype(jnp.float32))
    product = product * live[:, None, None]
    summed = jax.ops.segment_sum(product, block_col, num_segments=COL_BLOCKS)
    return summed.reshape(COL_PANEL, WIDTH)

def reference(node_features, layer_weight, output_grad, block_values, block_position, tile_count):
    projected = jnp.dot(node_features, layer_weight, preferred_element_type=jnp.float32).astype(jnp.bfloat16)
    grid_view = projected.reshape(GRID_ROWS, GRID_COLS, NODE_DEV, WIDTH)
    col_panels = jnp.transpose(grid_view, (1, 0, 2, 3)).reshape(GRID_COLS, COL_PANEL, WIDTH)

    def row_sum(row_index):

        def add_tile(running, col_index):
            part = forward_tile(block_values[row_index, col_index], block_position[row_index, col_index], tile_count[row_index, col_index], col_panels[col_index])
            return (running + rounded(part), None)
        running, unused = lax.scan(add_tile, jnp.zeros((ROW_PANEL, WIDTH), jnp.float32), jnp.arange(GRID_COLS, dtype=jnp.int32))
        return running
    pre_activation = lax.map(row_sum, jnp.arange(GRID_ROWS, dtype=jnp.int32)).reshape(NODES, WIDTH)
    node_output = jax.nn.elu(pre_activation).astype(jnp.bfloat16)
    upstream = (output_grad.astype(jnp.float32) * elu_slope(pre_activation)).astype(jnp.bfloat16)
    row_panels = upstream.reshape(GRID_ROWS, ROW_PANEL, WIDTH)

    def col_sum(col_index):

        def add_tile(running, row_index):
            part = backward_tile(block_values[row_index, col_index], block_position[row_index, col_index], tile_count[row_index, col_index], row_panels[row_index])
            return (running + rounded(part), None)
        running, unused = lax.scan(add_tile, jnp.zeros((COL_PANEL, WIDTH), jnp.float32), jnp.arange(GRID_ROWS, dtype=jnp.int32))
        return running
    col_grads = lax.map(col_sum, jnp.arange(GRID_COLS, dtype=jnp.int32))
    column_grad = jnp.transpose(col_grads.reshape(GRID_COLS, GRID_ROWS, NODE_DEV, WIDTH), (1, 0, 2, 3))
    column_grad = column_grad.reshape(NODES, WIDTH)
    input_grad = jnp.dot(column_grad, layer_weight.astype(jnp.float32).T, precision=lax.Precision.HIGHEST).astype(jnp.bfloat16)
    weight_grad = jnp.dot(node_features.astype(jnp.float32).T, column_grad, precision=lax.Precision.HIGHEST) * (1.0 / math.sqrt(NODES))
    return (node_output, input_grad, weight_grad)
```

```python
import functools
import math

import jax
import jax.numpy as jnp
from jax import lax
from jax.experimental import pallas as pl
from jax.experimental.pallas import tpu as pltpu
from jax.sharding import PartitionSpec as P

MESH = pl.DeviceIdType.MESH
F32 = jnp.float32
BF16 = jnp.bfloat16


def repeat(start, stop, step):
    if stop - start <= 8:
        for d in range(start, stop):
            step(d)
    else:

        def one(d, unused):
            step(d)
            return unused

        lax.fori_loop(start, stop, one, 0)


def split_dot(left, right, dims):
    high = left.astype(BF16)
    low = (left - high.astype(F32)).astype(BF16)
    first = lax.dot_general(high, right, dims, preferred_element_type=F32)
    return first + lax.dot_general(low, right, dims, preferred_element_type=F32)


def kernel(
    rows,
    cols,
    position,
    count,
    x_ref,
    w_ref,
    og_ref,
    values_hbm,
    out_ref,
    ig_ref,
    wg_ref,
    values,
    xg,
    tile,
    tile_t,
    part,
    part_in,
    up,
    acc,
    pc,
    pc_in,
    term,
    w1_in,
    own,
    w2_in,
    small,
    w3_in,
    w4_in,
    sem_v,
    sem_x,
    sem_p,
    sem_u,
    sem_c,
    sem_w1,
    sem_w2,
    sem_w3,
    sem_w4,
):
    nodes, width = x_ref.shape
    slots, block = values_hbm.shape[0], values_hbm.shape[1]
    col_blocks = rows
    my_row = lax.axis_index("row")
    my_col = lax.axis_index("col")
    size = {"row": rows, "col": cols}
    me = {"row": my_row, "col": my_col}

    def ahead(axis, d):
        return lax.rem(me[axis] + d, size[axis])

    def behind(axis, d):
        return lax.rem(me[axis] + size[axis] - d, size[axis])

    def send(axis, sem, d, src, dst):
        return pltpu.make_async_remote_copy(
            src_ref=src,
            dst_ref=dst,
            send_sem=sem.at[0, d - 1],
            recv_sem=sem.at[1, d - 1],
            device_id={axis: ahead(axis, d)},
            device_id_type=MESH,
        )

    load = pltpu.make_async_copy(values_hbm, values.at[pl.ds(0, slots)], sem_v)
    load.start()

    barrier = pltpu.get_barrier_semaphore()
    for axis in ("row", "col"):

        def greet(d, axis=axis):
            pl.semaphore_signal(
                barrier, inc=1, device_id={axis: ahead(axis, d)}, device_id_type=MESH
            )

        repeat(1, size[axis], greet)
    pl.semaphore_wait(barrier, rows + cols - 2)

    repeat(1, rows, lambda d: send("row", sem_x, d, x_ref, xg.at[my_row]).start())
    xg[my_row] = x_ref[...]

    values[slots] = jnp.zeros((block, block), BF16)
    load.wait()
    live_count = count[0]

    def build(q, pointer):
        for k in range(col_blocks):
            here = position[jnp.minimum(pointer, slots - 1)]
            live = (here == q * col_blocks + k) & (pointer < live_count)
            slot = jnp.where(live, pointer, slots)
            tile[q, :, pl.ds(k * block, block)] = values[slot]
            pointer = pointer + live.astype(jnp.int32)
        return pointer

    if cols <= 8:
        pointer = jnp.int32(0)
        for q in range(cols):
            pointer = build(q, pointer)
    else:
        lax.fori_loop(0, cols, build, jnp.int32(0))

    def from_row(d):
        slot = xg.at[behind("row", d)]
        send("row", sem_x, d, slot, slot).wait_recv()

    repeat(1, rows, from_row)
    panel = xg[...].reshape(rows * nodes, width)

    def forward(d):
        to = ahead("col", d)
        product = jnp.dot(tile[to], panel, preferred_element_type=F32)
        part[to] = product.astype(BF16)
        send("col", sem_p, d, part.at[to], part_in.at[my_col]).start()

    repeat(1, cols, forward)
    small_sum = jnp.dot(tile[my_col], panel, preferred_element_type=F32)
    own[...] = small_sum

    def turn(q):
        for k in range(col_blocks):
            tile_t[q, pl.ds(k * block, block), :] = tile[q, :, pl.ds(k * block, block)].T

    repeat(0, cols, turn)

    def add_part(d):
        slot = part_in.at[behind("col", d)]
        send("col", sem_p, d, slot, slot).wait_recv()
        own[...] += part_in[behind("col", d)].astype(F32)

    repeat(1, cols, add_part)
    mixed = own[...]
    pre = split_dot(mixed, w_ref[...], (((1,), (0,)), ((), ())))
    decay = jnp.exp(jnp.minimum(pre, 0.0))
    slope = jnp.where(pre > 0, 1.0, decay)
    up[my_col] = (og_ref[...].astype(F32) * slope).astype(BF16)
    repeat(1, cols, lambda d: send("col", sem_u, d, up.at[my_col], up.at[my_col]).start())
    out_ref[...] = jnp.where(pre > 0, pre, decay - 1.0).astype(BF16)

    scale = 1.0 / math.sqrt(nodes * rows * cols)
    share = width // rows
    over_nodes = (((0,), (0,)), ((), ()))
    upstream = up[my_col]
    term[...] = (split_dot(mixed, upstream, over_nodes) * scale).reshape(rows, share, width)
    repeat(1, rows, lambda d: send("row", sem_w1, d, term.at[ahead("row", d)], w1_in.at[my_row]).start())

    acc[...] = jnp.dot(tile_t[my_col], upstream, preferred_element_type=F32)

    def back(d):
        slot = up.at[behind("col", d)]
        send("col", sem_u, d, slot, slot).wait_recv()
        acc[...] += jnp.dot(
            tile_t[behind("col", d)], up[behind("col", d)], preferred_element_type=F32
        )

    repeat(1, cols // 2, back)

    small[...] = term[my_row]

    def add_w1(d):
        slot = w1_in.at[behind("row", d)]
        send("row", sem_w1, d, slot, slot).wait_recv()
        small[...] += w1_in[behind("row", d)]

    repeat(1, rows, add_w1)
    piece = share // cols
    scattered = piece >= 8 and piece % 8 == 0
    if scattered:

        def send_w2(d):
            src = small.at[pl.ds(pl.multiple_of(ahead("col", d) * piece, piece), piece)]
            send("col", sem_w2, d, src, w2_in.at[my_col]).start()
    else:

        def send_w2(d):
            send("col", sem_w2, d, small, w2_in.at[my_col]).start()

    repeat(1, cols, send_w2)
    repeat(cols // 2, cols, back)

    def scatter_cols(d):
        to = ahead("row", d)
        pc[to] = acc[pl.ds(pl.multiple_of(to * nodes, nodes), nodes), :].astype(BF16)
        send("row", sem_c, d, pc.at[to], pc_in.at[my_row]).start()

    repeat(1, rows, scatter_cols)

    def w2_wait(d):
        slot = w2_in.at[behind("col", d)]
        send("col", sem_w2, d, slot, slot).wait_recv()

    repeat(1, cols, w2_wait)
    if scattered:
        w2_in[my_col] = small[pl.ds(pl.multiple_of(my_col * piece, piece), piece), :]
        w3_in[my_col] = jnp.sum(w2_in[...], axis=0)
        repeat(1, cols, lambda d: send("col", sem_w3, d, w3_in.at[my_col], w3_in.at[my_col]).start())
    else:
        w2_in[my_col] = small[...]
        w4_in[my_row] = jnp.sum(w2_in[...], axis=0)

    grad = acc[pl.ds(pl.multiple_of(my_row * nodes, nodes), nodes), :]
    own[...] = grad

    def add_pc(d):
        slot = pc_in.at[behind("row", d)]
        send("row", sem_c, d, slot, slot).wait_recv()
        own[...] += pc_in[behind("row", d)].astype(F32)

    repeat(1, rows, add_pc)
    ig_ref[...] = split_dot(own[...], w_ref[...], (((1,), (1,)), ((), ()))).astype(BF16)

    if scattered:

        def w3_wait(d):
            slot = w3_in.at[behind("col", d)]
            send("col", sem_w3, d, slot, slot).wait_recv()

        repeat(1, cols, w3_wait)
        w4_in[my_row] = w3_in[...].reshape(share, width)
    repeat(1, rows, lambda d: send("row", sem_w4, d, w4_in.at[my_row], w4_in.at[my_row]).start())

    def w4_wait(d):
        slot = w4_in.at[behind("row", d)]
        send("row", sem_w4, d, slot, slot).wait_recv()

    repeat(1, rows, w4_wait)
    wg_ref[...] = w4_in[...].reshape(width, width)

    def row_sent(d):
        send("row", sem_x, d, x_ref, xg.at[my_row]).wait_send()
        send("row", sem_w1, d, term.at[my_row], w1_in.at[my_row]).wait_send()
        send("row", sem_c, d, pc.at[my_row], pc_in.at[my_row]).wait_send()
        send("row", sem_w4, d, w4_in.at[my_row], w4_in.at[my_row]).wait_send()

    def col_sent(d):
        send("col", sem_p, d, part.at[my_col], part_in.at[my_col]).wait_send()
        send("col", sem_u, d, up.at[my_col], up.at[my_col]).wait_send()
        if scattered:
            send("col", sem_w2, d, small.at[pl.ds(0, piece)], w2_in.at[my_col]).wait_send()
            send("col", sem_w3, d, w3_in.at[my_col], w3_in.at[my_col]).wait_send()
        else:
            send("col", sem_w2, d, small, w2_in.at[my_col]).wait_send()

    repeat(1, rows, row_sent)
    repeat(1, cols, col_sent)


def body(node_features, layer_weight, output_grad, block_values, block_position, tile_count):
    rows, cols = lax.axis_size("row"), lax.axis_size("col")
    nodes, width = node_features.shape
    slots, block = block_values.shape[2], block_values.shape[3]
    assert nodes == block
    share = width // rows
    piece = share // cols
    if not (piece >= 8 and piece % 8 == 0):
        piece = share
    vmem = pl.BlockSpec(memory_space=pltpu.VMEM)
    smem = pl.BlockSpec(memory_space=pltpu.SMEM)
    dma = pltpu.SemaphoreType.DMA
    return pl.pallas_call(
        functools.partial(kernel, rows, cols),
        out_shape=(
            jax.ShapeDtypeStruct((nodes, width), BF16),
            jax.ShapeDtypeStruct((nodes, width), BF16),
            jax.ShapeDtypeStruct((width, width), F32),
        ),
        in_specs=[smem, smem, vmem, vmem, vmem, pl.BlockSpec(memory_space=pl.ANY)],
        out_specs=(vmem, vmem, vmem),
        scratch_shapes=[
            pltpu.VMEM((slots + 1, block, block), BF16),
            pltpu.VMEM((rows, nodes, width), BF16),
            pltpu.VMEM((cols, nodes, rows * nodes), BF16),
            pltpu.VMEM((cols, rows * nodes, nodes), BF16),
            pltpu.VMEM((cols, nodes, width), BF16),
            pltpu.VMEM((cols, nodes, width), BF16),
            pltpu.VMEM((cols, nodes, width), BF16),
            pltpu.VMEM((rows * nodes, width), F32),
            pltpu.VMEM((rows, nodes, width), BF16),
            pltpu.VMEM((rows, nodes, width), BF16),
            pltpu.VMEM((rows, share, width), F32),
            pltpu.VMEM((rows, share, width), F32),
            pltpu.VMEM((nodes, width), F32),
            pltpu.VMEM((cols, piece, width), F32),
            pltpu.VMEM((share, width), F32),
            pltpu.VMEM((cols, piece, width), F32),
            pltpu.VMEM((rows, share, width), F32),
            dma,
            dma((2, rows - 1)),
            dma((2, cols - 1)),
            dma((2, cols - 1)),
            dma((2, rows - 1)),
            dma((2, rows - 1)),
            dma((2, cols - 1)),
            dma((2, cols - 1)),
            dma((2, rows - 1)),
        ],
        compiler_params=pltpu.CompilerParams(collective_id=0, has_side_effects=True),
    )(
        block_position.reshape(slots),
        tile_count.reshape(1),
        node_features,
        layer_weight,
        output_grad,
        block_values.reshape(slots, block, block),
    )


def solution(mesh):
    in_specs = (
        P(("row", "col"), None),
        P(),
        P(("row", "col"), None),
        P("row", "col", None, None, None),
        P("row", "col", None),
        P("row", "col"),
    )
    out_specs = (P(("row", "col"), None), P(("row", "col"), None), P())
    return jax.shard_map(body, mesh=mesh, in_specs=in_specs, out_specs=out_specs, check_vma=False)
```

```python
import functools
import math

import jax
import jax.numpy as jnp
from jax import lax
from jax.experimental import pallas as pl
from jax.experimental.pallas import tpu as pltpu
from jax.sharding import PartitionSpec as P

MESH = pl.DeviceIdType.MESH
F32 = jnp.float32
BF16 = jnp.bfloat16


def repeat(steps, step):
    if len(steps) <= 8:
        for d in steps:
            step(d)
    else:

        def one(d, unused):
            step(d)
            return unused

        lax.fori_loop(min(steps), max(steps) + 1, one, 0)


def split_dot(left, right, dims):
    high = left.astype(BF16)
    low = (left - high.astype(F32)).astype(BF16)
    first = lax.dot_general(high, right, dims, preferred_element_type=F32)
    return first + lax.dot_general(low, right, dims, preferred_element_type=F32)


def kernel(
    rows,
    cols,
    position,
    count,
    x_hbm,
    w_hbm,
    og_hbm,
    values_hbm,
    out_hbm,
    ig_hbm,
    wg_hbm,
    values,
    w_ref,
    og_ref,
    out_ref,
    ig_ref,
    wg_ref,
    xg,
    tile,
    tile_t,
    mate_part,
    mate_in,
    part,
    part_in,
    up,
    acc,
    pc,
    pc_in,
    term,
    w1_in,
    own,
    w2_in,
    small,
    w3_in,
    w4_in,
    sem_v,
    sem_x,
    sem_y,
    sem_z,
    sem_u,
    sem_f,
    sem_c,
    sem_w1,
    sem_w2,
    sem_w3,
    sem_w4,
):
    nodes, width = x_hbm.shape
    slots, block = values_hbm.shape[0], values_hbm.shape[1]
    col_blocks = rows
    my_row = lax.axis_index("row")
    my_col = lax.axis_index("col")
    size = {"row": rows, "col": cols}
    me = {"row": my_row, "col": my_col}
    half = cols // 2
    my_high = my_col // 2
    my_low = lax.rem(my_col, 2)
    mate = my_high * 2 + 1 - my_low
    others = [half // 2] + [d for d in range(1, half) if d != half // 2]
    row_steps = list(range(1, rows))
    col_steps = list(range(1, cols))

    def ahead(axis, d):
        return lax.rem(me[axis] + d, size[axis])

    def behind(axis, d):
        return lax.rem(me[axis] + size[axis] - d, size[axis])

    def high_ahead(d):
        return lax.rem(my_high + d, half)

    def high_behind(d):
        return lax.rem(my_high + half - d, half)

    def move(sem, index, src, dst, **target):
        return pltpu.make_async_remote_copy(
            src_ref=src,
            dst_ref=dst,
            send_sem=sem.at[0, index],
            recv_sem=sem.at[1, index],
            device_id=target,
            device_id_type=MESH,
        )

    def send(axis, sem, d, src, dst):
        return move(sem, d - 1, src, dst, **{axis: ahead(axis, d)})

    load = pltpu.make_async_copy(values_hbm, values.at[pl.ds(0, slots)], sem_v.at[0])
    load_x = pltpu.make_async_copy(x_hbm, xg.at[my_row], sem_v.at[1])
    load_w = pltpu.make_async_copy(w_hbm, w_ref, sem_v.at[2])
    load_og = pltpu.make_async_copy(og_hbm, og_ref, sem_v.at[3])
    for one in (load, load_x, load_w, load_og):
        one.start()

    barrier = pltpu.get_barrier_semaphore()
    for axis in ("col", "row"):

        def greet(d, axis=axis):
            pl.semaphore_signal(
                barrier, inc=1, device_id={axis: ahead(axis, d)}, device_id_type=MESH
            )

        repeat(list(range(1, size[axis])), greet)
    values[slots] = jnp.zeros((block, block), BF16)
    pl.semaphore_wait(barrier, rows + cols - 2)

    repeat(row_steps, lambda d: send("row", sem_x, d, x_hbm, xg.at[my_row]).start())

    load.wait()
    live_count = count[0, 0]

    def build(q, pointer):
        for k in range(col_blocks):
            here = position[jnp.minimum(pointer, slots - 1)]
            live = (here == q * col_blocks + k) & (pointer < live_count)
            slot = jnp.where(live, pointer, slots)
            tile[q, :, pl.ds(k * block, block)] = values[slot]
            pointer = pointer + live.astype(jnp.int32)
        return pointer

    if cols <= 8:
        pointer = jnp.int32(0)
        for q in range(cols):
            pointer = build(q, pointer)
    else:
        lax.fori_loop(0, cols, build, jnp.int32(0))

    load_x.wait()

    def from_row(d):
        slot = xg.at[behind("row", d)]
        send("row", sem_x, d, slot, slot).wait_recv()

    repeat(row_steps, from_row)
    panel = xg[...].reshape(rows * nodes, width)

    def to_mate(d):
        high = high_ahead(d)
        product = jnp.dot(tile[high * 2 + 1 - my_low], panel, preferred_element_type=F32)
        mate_part[high] = product.astype(BF16)
        move(sem_y, d, mate_part.at[high], mate_in.at[high], col=mate).start()

    repeat(others, to_mate)
    to_mate(0)

    def from_mate(d):
        high = high_ahead(d)
        product = jnp.dot(tile[high * 2 + my_low], panel, preferred_element_type=F32)
        slot = mate_in.at[high]
        move(sem_y, d, slot, slot, col=mate).wait_recv()
        return product + mate_in[high].astype(F32)

    def to_high(d):
        high = high_ahead(d)
        part[high] = from_mate(d).astype(BF16)
        move(sem_z, d - 1, part.at[high], part_in.at[my_high], col=high * 2 + my_low).start()

    repeat(others, to_high)
    own[...] = from_mate(0)

    def turn(q):
        for k in range(col_blocks):
            tile_t[q, pl.ds(k * block, block), :] = tile[q, :, pl.ds(k * block, block)].T

    repeat(list(range(cols)), turn)

    def add_part(d):
        high = high_behind(d)
        slot = part_in.at[high]
        move(sem_z, d - 1, slot, slot, col=high * 2 + my_low).wait_recv()
        own[...] += part_in[high].astype(F32)

    load_w.wait()
    load_og.wait()
    repeat(others, add_part)
    mixed = own[...]
    pre = split_dot(mixed, w_ref[...], (((1,), (0,)), ((), ())))
    decay = jnp.exp(jnp.minimum(pre, 0.0))
    slope = jnp.where(pre > 0, 1.0, decay)
    up[my_col] = (og_ref[...].astype(F32) * slope).astype(BF16)

    def up_high(d):
        move(sem_u, d - 1, up.at[my_col], up.at[my_col], col=high_ahead(d) * 2 + my_low).start()

    move(sem_f, 0, up.at[my_col], up.at[my_col], col=mate).start()
    repeat(others, up_high)
    out_ref[...] = jnp.where(pre > 0, pre, decay - 1.0).astype(BF16)
    save_out = pltpu.make_async_copy(out_ref, out_hbm, sem_v.at[4])
    save_out.start()

    scale = 1.0 / math.sqrt(nodes * rows * cols)
    share = width // rows
    over_nodes = (((0,), (0,)), ((), ()))
    upstream = up[my_col]
    term[...] = (split_dot(mixed, upstream, over_nodes) * scale).reshape(rows, share, width)
    repeat(
        row_steps,
        lambda d: send("row", sem_w1, d, term.at[ahead("row", d)], w1_in.at[my_row]).start(),
    )

    acc[...] = jnp.dot(tile_t[my_col], upstream, preferred_element_type=F32)

    def back(source):
        acc[...] += jnp.dot(tile_t[source], up[source], preferred_element_type=F32)

    def back_high(d):
        source = high_behind(d) * 2 + my_low
        slot = up.at[source]
        move(sem_u, d - 1, slot, slot, col=source).wait_recv()
        move(sem_f, d, slot, slot, col=mate).start()
        back(source)

    def back_mate(d):
        source = high_behind(d) * 2 + 1 - my_low
        slot = up.at[source]
        move(sem_f, d, slot, slot, col=mate).wait_recv()
        back(source)

    back_mate(0)

    small[...] = term[my_row]

    def add_w1(d):
        slot = w1_in.at[behind("row", d)]
        send("row", sem_w1, d, slot, slot).wait_recv()
        small[...] += w1_in[behind("row", d)]

    repeat(row_steps, add_w1)
    piece = share // cols
    scattered = piece >= 8 and piece % 8 == 0
    if scattered:

        def send_w2(d):
            src = small.at[pl.ds(pl.multiple_of(ahead("col", d) * piece, piece), piece)]
            send("col", sem_w2, d, src, w2_in.at[my_col]).start()
    else:

        def send_w2(d):
            send("col", sem_w2, d, small, w2_in.at[my_col]).start()

    repeat(col_steps, send_w2)

    def w2_wait(d):
        slot = w2_in.at[behind("col", d)]
        send("col", sem_w2, d, slot, slot).wait_recv()

    repeat(others, back_high)
    repeat(col_steps, w2_wait)
    if scattered:
        w2_in[my_col] = small[pl.ds(pl.multiple_of(my_col * piece, piece), piece), :]
        w3_in[my_col] = jnp.sum(w2_in[...], axis=0)
        repeat(
            col_steps,
            lambda d: send("col", sem_w3, d, w3_in.at[my_col], w3_in.at[my_col]).start(),
        )
    else:
        w2_in[my_col] = small[...]
        w4_in[my_row] = jnp.sum(w2_in[...], axis=0)

    repeat(others, back_mate)

    def scatter_cols(d):
        to = ahead("row", d)
        pc[to] = acc[pl.ds(pl.multiple_of(to * nodes, nodes), nodes), :].astype(BF16)
        send("row", sem_c, d, pc.at[to], pc_in.at[my_row]).start()

    repeat(row_steps, scatter_cols)

    if scattered:

        def w3_wait(d):
            slot = w3_in.at[behind("col", d)]
            send("col", sem_w3, d, slot, slot).wait_recv()

        repeat(col_steps, w3_wait)
        w4_in[my_row] = w3_in[...].reshape(share, width)
    repeat(
        row_steps, lambda d: send("row", sem_w4, d, w4_in.at[my_row], w4_in.at[my_row]).start()
    )

    own[...] = acc[pl.ds(pl.multiple_of(my_row * nodes, nodes), nodes), :]

    def add_pc(d):
        slot = pc_in.at[behind("row", d)]
        send("row", sem_c, d, slot, slot).wait_recv()
        own[...] += pc_in[behind("row", d)].astype(F32)

    repeat(row_steps, add_pc)
    ig_ref[...] = split_dot(own[...], w_ref[...], (((1,), (1,)), ((), ()))).astype(BF16)
    save_ig = pltpu.make_async_copy(ig_ref, ig_hbm, sem_v.at[5])
    save_ig.start()

    def row_sent(d):
        send("row", sem_x, d, x_hbm, xg.at[my_row]).wait_send()
        send("row", sem_w1, d, term.at[my_row], w1_in.at[my_row]).wait_send()
        send("row", sem_c, d, pc.at[my_row], pc_in.at[my_row]).wait_send()
        send("row", sem_w4, d, w4_in.at[my_row], w4_in.at[my_row]).wait_send()

    def col_sent(d):
        if scattered:
            send("col", sem_w2, d, small.at[pl.ds(0, piece)], w2_in.at[my_col]).wait_send()
            send("col", sem_w3, d, w3_in.at[my_col], w3_in.at[my_col]).wait_send()
        else:
            send("col", sem_w2, d, small, w2_in.at[my_col]).wait_send()

    def mate_sent(d):
        move(sem_y, d, mate_part.at[0], mate_in.at[0], col=mate).wait_send()
        move(sem_f, d, up.at[my_col], up.at[my_col], col=mate).wait_send()

    def high_sent(d):
        move(sem_z, d - 1, part.at[0], part_in.at[0], col=mate).wait_send()
        move(sem_u, d - 1, up.at[my_col], up.at[my_col], col=mate).wait_send()

    repeat(list(range(half)), mate_sent)
    repeat(list(range(1, half)), high_sent)
    repeat(col_steps, col_sent)

    def w4_wait(d):
        slot = w4_in.at[behind("row", d)]
        send("row", sem_w4, d, slot, slot).wait_recv()

    repeat(row_steps, w4_wait)
    wg_ref[...] = w4_in[...].reshape(width, width)
    save_wg = pltpu.make_async_copy(wg_ref, wg_hbm, sem_v.at[6])
    save_wg.start()
    repeat(row_steps, row_sent)
    save_out.wait()
    save_ig.wait()
    save_wg.wait()


def body(node_features, layer_weight, output_grad, block_values, block_position, tile_count):
    rows, cols = lax.axis_size("row"), lax.axis_size("col")
    nodes, width = node_features.shape
    slots, block = block_values.shape[2], block_values.shape[3]
    assert nodes == block
    share = width // rows
    piece = share // cols
    if not (piece >= 8 and piece % 8 == 0):
        piece = share
    place = pl.BlockSpec(memory_space=pl.ANY)
    half = cols // 2
    assert cols == 2 * half
    smem = pl.BlockSpec(memory_space=pltpu.SMEM)
    dma = pltpu.SemaphoreType.DMA
    return pl.pallas_call(
        functools.partial(kernel, rows, cols),
        out_shape=(
            jax.ShapeDtypeStruct((nodes, width), BF16),
            jax.ShapeDtypeStruct((nodes, width), BF16),
            jax.ShapeDtypeStruct((width, width), F32),
        ),
        in_specs=[smem, smem, place, place, place, place],
        out_specs=(place, place, place),
        scratch_shapes=[
            pltpu.VMEM((slots + 1, block, block), BF16),
            pltpu.VMEM((width, width), BF16),
            pltpu.VMEM((nodes, width), BF16),
            pltpu.VMEM((nodes, width), BF16),
            pltpu.VMEM((nodes, width), BF16),
            pltpu.VMEM((width, width), F32),
            pltpu.VMEM((rows, nodes, width), BF16),
            pltpu.VMEM((cols, nodes, rows * nodes), BF16),
            pltpu.VMEM((cols, rows * nodes, nodes), BF16),
            pltpu.VMEM((half, nodes, width), BF16),
            pltpu.VMEM((half, nodes, width), BF16),
            pltpu.VMEM((half, nodes, width), BF16),
            pltpu.VMEM((half, nodes, width), BF16),
            pltpu.VMEM((cols, nodes, width), BF16),
            pltpu.VMEM((rows * nodes, width), F32),
            pltpu.VMEM((rows, nodes, width), BF16),
            pltpu.VMEM((rows, nodes, width), BF16),
            pltpu.VMEM((rows, share, width), F32),
            pltpu.VMEM((rows, share, width), F32),
            pltpu.VMEM((nodes, width), F32),
            pltpu.VMEM((cols, piece, width), F32),
            pltpu.VMEM((share, width), F32),
            pltpu.VMEM((cols, piece, width), F32),
            pltpu.VMEM((rows, share, width), F32),
            dma((7,)),
            dma((2, rows - 1)),
            dma((2, half)),
            dma((2, half - 1)),
            dma((2, half - 1)),
            dma((2, half)),
            dma((2, rows - 1)),
            dma((2, rows - 1)),
            dma((2, cols - 1)),
            dma((2, cols - 1)),
            dma((2, rows - 1)),
        ],
        compiler_params=pltpu.CompilerParams(collective_id=0, has_side_effects=True),
    )(
        block_position.reshape(slots),
        tile_count,
        node_features,
        layer_weight,
        output_grad,
        block_values.reshape(slots, block, block),
    )


def solution(mesh):
    in_specs = (
        P(("row", "col"), None),
        P(),
        P(("row", "col"), None),
        P("row", "col", None, None, None),
        P("row", "col", None),
        P("row", "col"),
    )
    out_specs = (P(("row", "col"), None), P(("row", "col"), None), P())
    return jax.shard_map(body, mesh=mesh, in_specs=in_specs, out_specs=out_specs, check_vma=False)
```

```python
import functools
import math

import jax
import jax.numpy as jnp
from jax import lax
from jax.experimental import pallas as pl
from jax.experimental.pallas import tpu as pltpu
from jax.sharding import PartitionSpec as P

MESH = pl.DeviceIdType.MESH
F32 = jnp.float32
BF16 = jnp.bfloat16


def repeat(steps, step):
    if len(steps) <= 8:
        for d in steps:
            step(d)
    else:

        def one(d, unused):
            step(d)
            return unused

        lax.fori_loop(min(steps), max(steps) + 1, one, 0)


def split_dot(left, right, dims):
    high = left.astype(BF16)
    low = (left - high.astype(F32)).astype(BF16)
    first = lax.dot_general(high, right, dims, preferred_element_type=F32)
    return first + lax.dot_general(low, right, dims, preferred_element_type=F32)


def kernel(
    rows,
    cols,
    position,
    count,
    x_hbm,
    w_hbm,
    og_hbm,
    values_hbm,
    out_ref,
    ig_ref,
    wg_ref,
    values,
    w_ref,
    og_ref,
    xg,
    tile,
    tile_t,
    mate_part,
    mate_in,
    part,
    part_in,
    up,
    acc,
    pc,
    pc_in,
    term,
    w1_in,
    own,
    w2_in,
    small,
    w3_in,
    w4_in,
    sem_v,
    sem_x,
    sem_y,
    sem_z,
    sem_u,
    sem_f,
    sem_c,
    sem_w1,
    sem_w2,
    sem_w3,
    sem_w4,
):
    nodes, width = x_hbm.shape
    slots, block = values_hbm.shape[0], values_hbm.shape[1]
    col_blocks = rows
    my_row = lax.axis_index("row")
    my_col = lax.axis_index("col")
    size = {"row": rows, "col": cols}
    me = {"row": my_row, "col": my_col}
    half = cols // 2
    my_high = my_col // 2
    my_low = lax.rem(my_col, 2)
    mate = my_high * 2 + 1 - my_low
    others = [half // 2] + [d for d in range(1, half) if d != half // 2]
    row_steps = list(range(1, rows))
    col_steps = list(range(1, cols))

    def ahead(axis, d):
        return lax.rem(me[axis] + d, size[axis])

    def behind(axis, d):
        return lax.rem(me[axis] + size[axis] - d, size[axis])

    def high_ahead(d):
        return lax.rem(my_high + d, half)

    def high_behind(d):
        return lax.rem(my_high + half - d, half)

    def move(sem, index, src, dst, **target):
        return pltpu.make_async_remote_copy(
            src_ref=src,
            dst_ref=dst,
            send_sem=sem.at[0, index],
            recv_sem=sem.at[1, index],
            device_id=target,
            device_id_type=MESH,
        )

    def send(axis, sem, d, src, dst):
        return move(sem, d - 1, src, dst, **{axis: ahead(axis, d)})

    load = pltpu.make_async_copy(values_hbm, values.at[pl.ds(0, slots)], sem_v.at[0])
    load_x = pltpu.make_async_copy(x_hbm, xg.at[my_row], sem_v.at[1])
    load_w = pltpu.make_async_copy(w_hbm, w_ref, sem_v.at[2])
    load_og = pltpu.make_async_copy(og_hbm, og_ref, sem_v.at[3])
    for one in (load, load_x, load_w, load_og):
        one.start()

    barrier = pltpu.get_barrier_semaphore()
    for axis in ("col", "row"):

        def greet(d, axis=axis):
            pl.semaphore_signal(
                barrier, inc=1, device_id={axis: ahead(axis, d)}, device_id_type=MESH
            )

        repeat(list(range(1, size[axis])), greet)
    values[slots] = jnp.zeros((block, block), BF16)
    pl.semaphore_wait(barrier, rows + cols - 2)

    repeat(row_steps, lambda d: send("row", sem_x, d, x_hbm, xg.at[my_row]).start())

    load.wait()
    live_count = count[0, 0]

    def build(q, pointer):
        for k in range(col_blocks):
            here = position[jnp.minimum(pointer, slots - 1)]
            live = (here == q * col_blocks + k) & (pointer < live_count)
            slot = jnp.where(live, pointer, slots)
            tile[q, :, pl.ds(k * block, block)] = values[slot]
            pointer = pointer + live.astype(jnp.int32)
        return pointer

    if cols <= 8:
        pointer = jnp.int32(0)
        for q in range(cols):
            pointer = build(q, pointer)
    else:
        lax.fori_loop(0, cols, build, jnp.int32(0))

    load_x.wait()

    def from_row(d):
        slot = xg.at[behind("row", d)]
        send("row", sem_x, d, slot, slot).wait_recv()

    repeat(row_steps, from_row)
    panel = xg[...].reshape(rows * nodes, width)

    def to_mate(d):
        high = high_ahead(d)
        product = jnp.dot(tile[high * 2 + 1 - my_low], panel, preferred_element_type=F32)
        mate_part[high] = product.astype(BF16)
        move(sem_y, d, mate_part.at[high], mate_in.at[high], col=mate).start()

    repeat(others, to_mate)
    to_mate(0)

    def from_mate(d):
        high = high_ahead(d)
        product = jnp.dot(tile[high * 2 + my_low], panel, preferred_element_type=F32)
        slot = mate_in.at[high]
        move(sem_y, d, slot, slot, col=mate).wait_recv()
        return product + mate_in[high].astype(F32)

    def to_high(d):
        high = high_ahead(d)
        part[high] = from_mate(d).astype(BF16)
        move(sem_z, d - 1, part.at[high], part_in.at[my_high], col=high * 2 + my_low).start()

    repeat(others, to_high)
    own[...] = from_mate(0)

    def turn(q):
        for k in range(col_blocks):
            tile_t[q, pl.ds(k * block, block), :] = tile[q, :, pl.ds(k * block, block)].T

    repeat(list(range(cols)), turn)

    def add_part(d):
        high = high_behind(d)
        slot = part_in.at[high]
        move(sem_z, d - 1, slot, slot, col=high * 2 + my_low).wait_recv()
        own[...] += part_in[high].astype(F32)

    load_w.wait()
    load_og.wait()
    repeat(others, add_part)
    mixed = own[...]
    pre = split_dot(mixed, w_ref[...], (((1,), (0,)), ((), ())))
    decay = jnp.exp(jnp.minimum(pre, 0.0))
    slope = jnp.where(pre > 0, 1.0, decay)
    up[my_col] = (og_ref[...].astype(F32) * slope).astype(BF16)

    def up_high(d):
        move(sem_u, d - 1, up.at[my_col], up.at[my_col], col=high_ahead(d) * 2 + my_low).start()

    move(sem_f, 0, up.at[my_col], up.at[my_col], col=mate).start()
    repeat(others, up_high)
    out_ref[...] = jnp.where(pre > 0, pre, decay - 1.0).astype(BF16)

    scale = 1.0 / math.sqrt(nodes * rows * cols)
    share = width // rows
    over_nodes = (((0,), (0,)), ((), ()))
    upstream = up[my_col]
    term[...] = (split_dot(mixed, upstream, over_nodes) * scale).reshape(rows, share, width).astype(BF16)
    repeat(
        row_steps,
        lambda d: send("row", sem_w1, d, term.at[ahead("row", d)], w1_in.at[my_row]).start(),
    )

    acc[...] = jnp.dot(tile_t[my_col], upstream, preferred_element_type=F32)

    def back(source):
        acc[...] += jnp.dot(tile_t[source], up[source], preferred_element_type=F32)

    def back_high(d):
        source = high_behind(d) * 2 + my_low
        slot = up.at[source]
        move(sem_u, d - 1, slot, slot, col=source).wait_recv()
        move(sem_f, d, slot, slot, col=mate).start()
        back(source)

    def back_mate(d):
        source = high_behind(d) * 2 + 1 - my_low
        slot = up.at[source]
        move(sem_f, d, slot, slot, col=mate).wait_recv()
        back(source)

    back_mate(0)

    small[...] = term[my_row].astype(F32)

    def add_w1(d):
        slot = w1_in.at[behind("row", d)]
        send("row", sem_w1, d, slot, slot).wait_recv()
        small[...] += w1_in[behind("row", d)].astype(F32)

    repeat(row_steps, add_w1)
    piece = share // cols
    scattered = piece >= 8 and piece % 8 == 0
    if scattered:

        def send_w2(d):
            src = small.at[pl.ds(pl.multiple_of(ahead("col", d) * piece, piece), piece)]
            send("col", sem_w2, d, src, w2_in.at[my_col]).start()
    else:

        def send_w2(d):
            send("col", sem_w2, d, small, w2_in.at[my_col]).start()

    repeat(col_steps, send_w2)

    def w2_wait(d):
        slot = w2_in.at[behind("col", d)]
        send("col", sem_w2, d, slot, slot).wait_recv()

    repeat(others, back_high)
    repeat(col_steps, w2_wait)
    if scattered:
        w2_in[my_col] = small[pl.ds(pl.multiple_of(my_col * piece, piece), piece), :]
        w3_in[my_col] = jnp.sum(w2_in[...], axis=0)
        repeat(
            col_steps,
            lambda d: send("col", sem_w3, d, w3_in.at[my_col], w3_in.at[my_col]).start(),
        )
    else:
        w2_in[my_col] = small[...]
        w4_in[my_row] = jnp.sum(w2_in[...], axis=0).astype(BF16)

    repeat(others, back_mate)

    def scatter_cols(d):
        to = ahead("row", d)
        pc[to] = acc[pl.ds(pl.multiple_of(to * nodes, nodes), nodes), :].astype(BF16)
        send("row", sem_c, d, pc.at[to], pc_in.at[my_row]).start()

    repeat(row_steps, scatter_cols)

    if scattered:

        def w3_wait(d):
            slot = w3_in.at[behind("col", d)]
            send("col", sem_w3, d, slot, slot).wait_recv()

        repeat(col_steps, w3_wait)
        w4_in[my_row] = w3_in[...].reshape(share, width).astype(BF16)
    repeat(
        row_steps, lambda d: send("row", sem_w4, d, w4_in.at[my_row], w4_in.at[my_row]).start()
    )

    own[...] = acc[pl.ds(pl.multiple_of(my_row * nodes, nodes), nodes), :]

    def add_pc(d):
        slot = pc_in.at[behind("row", d)]
        send("row", sem_c, d, slot, slot).wait_recv()
        own[...] += pc_in[behind("row", d)].astype(F32)

    repeat(row_steps, add_pc)
    ig_ref[...] = split_dot(own[...], w_ref[...], (((1,), (1,)), ((), ()))).astype(BF16)

    def row_sent(d):
        send("row", sem_x, d, x_hbm, xg.at[my_row]).wait_send()
        send("row", sem_w1, d, term.at[my_row], w1_in.at[my_row]).wait_send()
        send("row", sem_c, d, pc.at[my_row], pc_in.at[my_row]).wait_send()
        send("row", sem_w4, d, w4_in.at[my_row], w4_in.at[my_row]).wait_send()

    def col_sent(d):
        if scattered:
            send("col", sem_w2, d, small.at[pl.ds(0, piece)], w2_in.at[my_col]).wait_send()
            send("col", sem_w3, d, w3_in.at[my_col], w3_in.at[my_col]).wait_send()
        else:
            send("col", sem_w2, d, small, w2_in.at[my_col]).wait_send()

    def mate_sent(d):
        move(sem_y, d, mate_part.at[0], mate_in.at[0], col=mate).wait_send()
        move(sem_f, d, up.at[my_col], up.at[my_col], col=mate).wait_send()

    def high_sent(d):
        move(sem_z, d - 1, part.at[0], part_in.at[0], col=mate).wait_send()
        move(sem_u, d - 1, up.at[my_col], up.at[my_col], col=mate).wait_send()

    repeat(list(range(half)), mate_sent)
    repeat(list(range(1, half)), high_sent)
    repeat(col_steps, col_sent)

    def w4_wait(d):
        slot = w4_in.at[behind("row", d)]
        send("row", sem_w4, d, slot, slot).wait_recv()

    repeat(row_steps, w4_wait)
    wg_ref[...] = w4_in[...].reshape(width, width).astype(F32)
    repeat(row_steps, row_sent)


def finish(out_ref, ig_ref, wg_ref, out_hbm, ig_hbm, wg_hbm, sem):
    trio = ((out_ref, out_hbm), (ig_ref, ig_hbm), (wg_ref, wg_hbm))
    copies = [pltpu.make_async_copy(a, b, sem.at[i]) for i, (a, b) in enumerate(trio)]
    for copy in copies:
        copy.start()
    for copy in copies:
        copy.wait()


def body(node_features, layer_weight, output_grad, block_values, block_position, tile_count):
    rows, cols = lax.axis_size("row"), lax.axis_size("col")
    nodes, width = node_features.shape
    slots, block = block_values.shape[2], block_values.shape[3]
    assert nodes == block
    share = width // rows
    piece = share // cols
    if not (piece >= 8 and piece % 8 == 0):
        piece = share
    place = pl.BlockSpec(memory_space=pl.ANY)
    inside = pl.BlockSpec(memory_space=pltpu.VMEM)
    half = cols // 2
    assert cols == 2 * half
    smem = pl.BlockSpec(memory_space=pltpu.SMEM)
    dma = pltpu.SemaphoreType.DMA
    shapes = (
        jax.ShapeDtypeStruct((nodes, width), BF16),
        jax.ShapeDtypeStruct((nodes, width), BF16),
        jax.ShapeDtypeStruct((width, width), F32),
    )
    results = pl.pallas_call(
        functools.partial(kernel, rows, cols),
        out_shape=(
            pltpu.VMEM((nodes, width), BF16),
            pltpu.VMEM((nodes, width), BF16),
            pltpu.VMEM((width, width), F32),
        ),
        in_specs=[smem, smem, place, place, place, place],
        out_specs=(inside, inside, inside),
        scratch_shapes=[
            pltpu.VMEM((slots + 1, block, block), BF16),
            pltpu.VMEM((width, width), BF16),
            pltpu.VMEM((nodes, width), BF16),
            pltpu.VMEM((rows, nodes, width), BF16),
            pltpu.VMEM((cols, nodes, rows * nodes), BF16),
            pltpu.VMEM((cols, rows * nodes, nodes), BF16),
            pltpu.VMEM((half, nodes, width), BF16),
            pltpu.VMEM((half, nodes, width), BF16),
            pltpu.VMEM((half, nodes, width), BF16),
            pltpu.VMEM((half, nodes, width), BF16),
            pltpu.VMEM((cols, nodes, width), BF16),
            pltpu.VMEM((rows * nodes, width), F32),
            pltpu.VMEM((rows, nodes, width), BF16),
            pltpu.VMEM((rows, nodes, width), BF16),
            pltpu.VMEM((rows, share, width), BF16),
            pltpu.VMEM((rows, share, width), BF16),
            pltpu.VMEM((nodes, width), F32),
            pltpu.VMEM((cols, piece, width), F32),
            pltpu.VMEM((share, width), F32),
            pltpu.VMEM((cols, piece, width), F32),
            pltpu.VMEM((rows, share, width), BF16),
            dma((7,)),
            dma((2, rows - 1)),
            dma((2, half)),
            dma((2, half - 1)),
            dma((2, half - 1)),
            dma((2, half)),
            dma((2, rows - 1)),
            dma((2, rows - 1)),
            dma((2, cols - 1)),
            dma((2, cols - 1)),
            dma((2, rows - 1)),
        ],
        compiler_params=pltpu.CompilerParams(collective_id=0, has_side_effects=True),
    )(
        block_position.reshape(slots),
        tile_count,
        node_features,
        layer_weight,
        output_grad,
        block_values.reshape(slots, block, block),
    )
    return pl.pallas_call(
        finish,
        out_shape=shapes,
        in_specs=[inside] * 3,
        out_specs=(place,) * 3,
        scratch_shapes=[
            dma((3,)),
        ],
        compiler_params=pltpu.CompilerParams(vmem_limit_bytes=4 << 20),
    )(*results)


def solution(mesh):
    in_specs = (
        P(("row", "col"), None),
        P(),
        P(("row", "col"), None),
        P("row", "col", None, None, None),
        P("row", "col", None),
        P("row", "col"),
    )
    out_specs = (P(("row", "col"), None), P(("row", "col"), None), P())
    return jax.shard_map(body, mesh=mesh, in_specs=in_specs, out_specs=out_specs, check_vma=False)
```

```python
import functools
import math

import jax
import jax.numpy as jnp
from jax import lax
from jax.experimental import pallas as pl
from jax.experimental.pallas import tpu as pltpu
from jax.sharding import PartitionSpec as P

MESH = pl.DeviceIdType.MESH
F32 = jnp.float32
BF16 = jnp.bfloat16


def repeat(steps, step):
    if len(steps) <= 8:
        for d in steps:
            step(d)
    else:

        def one(d, unused):
            step(d)
            return unused

        lax.fori_loop(min(steps), max(steps) + 1, one, 0)


def split_dot(left, right, dims):
    high = left.astype(BF16)
    low = (left - high.astype(F32)).astype(BF16)
    first = lax.dot_general(high, right, dims, preferred_element_type=F32)
    return first + lax.dot_general(low, right, dims, preferred_element_type=F32)


def kernel(
    rows,
    cols,
    position_hbm,
    count_hbm,
    x_hbm,
    w_hbm,
    og_hbm,
    values_hbm,
    out_ref,
    ig_ref,
    wg_ref,
    position,
    count,
    values,
    w_ref,
    og_ref,
    xg,
    tile,
    tile_t,
    mate_part,
    mate_in,
    part,
    part_in,
    up,
    acc,
    pc,
    pc_in,
    term,
    w1_in,
    own,
    w2_in,
    small,
    w3_in,
    w4_in,
    sem_v,
    sem_x,
    sem_y,
    sem_z,
    sem_u,
    sem_f,
    sem_c,
    sem_w1,
    sem_w2,
    sem_w3,
    sem_w4,
):
    nodes, width = x_hbm.shape
    slots, block = values_hbm.shape[0], values_hbm.shape[1]
    col_blocks = rows
    my_row = lax.axis_index("row")
    my_col = lax.axis_index("col")
    size = {"row": rows, "col": cols}
    me = {"row": my_row, "col": my_col}
    half = cols // 2
    my_high = my_col // 2
    my_low = lax.rem(my_col, 2)
    mate = my_high * 2 + 1 - my_low
    others = [half // 2] + [d for d in range(1, half) if d != half // 2]
    pieces = [pl.ds(p * nodes // 2, nodes // 2) for p in range(2)]
    count_pieces = len(pieces)
    row_steps = list(range(1, rows))
    col_steps = list(range(1, cols))

    def ahead(axis, d):
        return lax.rem(me[axis] + d, size[axis])

    def behind(axis, d):
        return lax.rem(me[axis] + size[axis] - d, size[axis])

    def high_ahead(d):
        return lax.rem(my_high + d, half)

    def high_behind(d):
        return lax.rem(my_high + half - d, half)

    def move(sem, index, src, dst, **target):
        return pltpu.make_async_remote_copy(
            src_ref=src,
            dst_ref=dst,
            send_sem=sem.at[0, index],
            recv_sem=sem.at[1, index],
            device_id=target,
            device_id_type=MESH,
        )

    def send(axis, sem, d, src, dst):
        return move(sem, d - 1, src, dst, **{axis: ahead(axis, d)})

    load = pltpu.make_async_copy(values_hbm, values.at[pl.ds(0, slots)], sem_v.at[0])
    load_x = pltpu.make_async_copy(x_hbm, xg.at[my_row], sem_v.at[1])
    load_w = pltpu.make_async_copy(w_hbm, w_ref, sem_v.at[2])
    load_og = pltpu.make_async_copy(og_hbm, og_ref, sem_v.at[3])
    load_position = pltpu.make_async_copy(position_hbm, position, sem_v.at[4])
    load_count = pltpu.make_async_copy(count_hbm, count, sem_v.at[5])
    for one in (load_position, load_count, load, load_x, load_w, load_og):
        one.start()

    barrier = pltpu.get_barrier_semaphore()

    def greet(**target):
        pl.semaphore_signal(barrier, inc=1, device_id=target, device_id_type=MESH)

    repeat(others, lambda d: greet(col=high_ahead(d) * 2 + my_low))
    greet(col=mate)
    repeat(row_steps, lambda d: greet(row=ahead("row", d)))
    values[slots] = jnp.zeros((block, block), BF16)
    pl.semaphore_wait(barrier, rows + half - 1)

    repeat(row_steps, lambda d: send("row", sem_x, d, x_hbm, xg.at[my_row]).start())

    load_position.wait()
    load_count.wait()
    load.wait()
    live_count = count[0, 0]

    def build(q, pointer):
        for k in range(col_blocks):
            here = position[jnp.minimum(pointer, slots - 1)]
            live = (here == q * col_blocks + k) & (pointer < live_count)
            slot = jnp.where(live, pointer, slots)
            tile[q, :, pl.ds(k * block, block)] = values[slot]
            pointer = pointer + live.astype(jnp.int32)
        return pointer

    if cols <= 8:
        pointer = jnp.int32(0)
        for q in range(cols):
            pointer = build(q, pointer)
    else:
        lax.fori_loop(0, cols, build, jnp.int32(0))

    load_x.wait()

    def from_row(d):
        slot = xg.at[behind("row", d)]
        send("row", sem_x, d, slot, slot).wait_recv()

    repeat(row_steps, from_row)
    panel = xg[...].reshape(rows * nodes, width)

    def to_mate(d):
        high = high_ahead(d)
        product = jnp.dot(tile[high * 2 + 1 - my_low], panel, preferred_element_type=F32)
        mate_part[high] = product.astype(BF16)
        for p, some in enumerate(pieces):
            index = d * count_pieces + p
            move(sem_y, index, mate_part.at[high, some], mate_in.at[high, some], col=mate).start()

    repeat(others, to_mate)
    to_mate(0)

    def from_mate(d, take):
        high = high_ahead(d)
        own[...] = jnp.dot(tile[high * 2 + my_low], panel, preferred_element_type=F32)
        for p, some in enumerate(pieces):
            slot = mate_in.at[high, some]
            move(sem_y, d * count_pieces + p, slot, slot, col=mate).wait_recv()
            take(p, some, own[some] + mate_in[high, some].astype(F32))

    def to_high(d):
        high = high_ahead(d)

        def take(p, some, total):
            part[high, some] = total.astype(BF16)
            move(
                sem_z,
                (d - 1) * count_pieces + p,
                part.at[high, some],
                part_in.at[my_high, some],
                col=high * 2 + my_low,
            ).start()

        from_mate(d, take)

    def keep(p, some, total):
        own[some] = total

    repeat(others, to_high)
    from_mate(0, keep)

    def turn(q):
        for k in range(col_blocks):
            tile_t[q, pl.ds(k * block, block), :] = tile[q, :, pl.ds(k * block, block)].T

    repeat(list(range(cols)), turn)

    def add_part(d):
        high = high_behind(d)
        for p, some in enumerate(pieces):
            slot = part_in.at[high, some]
            index = (d - 1) * count_pieces + p
            move(sem_z, index, slot, slot, col=high * 2 + my_low).wait_recv()
        own[...] += part_in[high].astype(F32)

    load_w.wait()
    load_og.wait()
    repeat(others, add_part)
    mixed = own[...]
    pre = split_dot(mixed, w_ref[...], (((1,), (0,)), ((), ())))
    decay = jnp.exp(jnp.minimum(pre, 0.0))
    slope = jnp.where(pre > 0, 1.0, decay)
    up[my_col] = (og_ref[...].astype(F32) * slope).astype(BF16)

    def up_high(d):
        for p, some in enumerate(pieces):
            mine = up.at[my_col, some]
            index = (d - 1) * count_pieces + p
            move(sem_u, index, mine, mine, col=high_ahead(d) * 2 + my_low).start()

    for p, some in enumerate(pieces):
        move(sem_f, p, up.at[my_col, some], up.at[my_col, some], col=mate).start()
    repeat(others, up_high)
    out_ref[...] = jnp.where(pre > 0, pre, decay - 1.0).astype(BF16)

    scale = 1.0 / math.sqrt(nodes * rows * cols)
    share = width // rows
    over_nodes = (((0,), (0,)), ((), ()))
    upstream = up[my_col]
    term[...] = (split_dot(mixed, upstream, over_nodes) * scale).reshape(rows, share, width).astype(BF16)
    repeat(
        row_steps,
        lambda d: send("row", sem_w1, d, term.at[ahead("row", d)], w1_in.at[my_row]).start(),
    )

    acc[...] = jnp.dot(tile_t[my_col], upstream, preferred_element_type=F32)

    def back(source):
        acc[...] += jnp.dot(tile_t[source], up[source], preferred_element_type=F32)

    def back_high(d):
        source = high_behind(d) * 2 + my_low
        for p, some in enumerate(pieces):
            slot = up.at[source, some]
            move(sem_u, (d - 1) * count_pieces + p, slot, slot, col=source).wait_recv()
            move(sem_f, d * count_pieces + p, slot, slot, col=mate).start()
        back(source)

    def back_mate(d):
        source = high_behind(d) * 2 + 1 - my_low
        for p, some in enumerate(pieces):
            slot = up.at[source, some]
            move(sem_f, d * count_pieces + p, slot, slot, col=mate).wait_recv()
        back(source)

    back_mate(0)

    small[...] = term[my_row].astype(F32)

    def add_w1(d):
        slot = w1_in.at[behind("row", d)]
        send("row", sem_w1, d, slot, slot).wait_recv()
        small[...] += w1_in[behind("row", d)].astype(F32)

    repeat(row_steps, add_w1)
    piece = share // cols
    scattered = piece >= 8 and piece % 8 == 0
    if scattered:

        def send_w2(d):
            src = small.at[pl.ds(pl.multiple_of(ahead("col", d) * piece, piece), piece)]
            send("col", sem_w2, d, src, w2_in.at[my_col]).start()
    else:

        def send_w2(d):
            send("col", sem_w2, d, small, w2_in.at[my_col]).start()

    repeat(col_steps, send_w2)

    def w2_wait(d):
        slot = w2_in.at[behind("col", d)]
        send("col", sem_w2, d, slot, slot).wait_recv()

    repeat(others, back_high)
    repeat(col_steps, w2_wait)
    if scattered:
        w2_in[my_col] = small[pl.ds(pl.multiple_of(my_col * piece, piece), piece), :]
        w3_in[my_col] = jnp.sum(w2_in[...], axis=0)
        repeat(
            col_steps,
            lambda d: send("col", sem_w3, d, w3_in.at[my_col], w3_in.at[my_col]).start(),
        )
    else:
        w2_in[my_col] = small[...]
        w4_in[my_row] = jnp.sum(w2_in[...], axis=0).astype(BF16)

    repeat(others, back_mate)

    def scatter_cols(d):
        to = ahead("row", d)
        pc[to] = acc[pl.ds(pl.multiple_of(to * nodes, nodes), nodes), :].astype(BF16)
        send("row", sem_c, d, pc.at[to], pc_in.at[my_row]).start()

    repeat(row_steps, scatter_cols)

    if scattered:

        def w3_wait(d):
            slot = w3_in.at[behind("col", d)]
            send("col", sem_w3, d, slot, slot).wait_recv()

        repeat(col_steps, w3_wait)
        w4_in[my_row] = w3_in[...].reshape(share, width).astype(BF16)
    repeat(
        row_steps, lambda d: send("row", sem_w4, d, w4_in.at[my_row], w4_in.at[my_row]).start()
    )

    own[...] = acc[pl.ds(pl.multiple_of(my_row * nodes, nodes), nodes), :]

    def add_pc(d):
        slot = pc_in.at[behind("row", d)]
        send("row", sem_c, d, slot, slot).wait_recv()
        own[...] += pc_in[behind("row", d)].astype(F32)

    repeat(row_steps, add_pc)
    ig_ref[...] = split_dot(own[...], w_ref[...], (((1,), (1,)), ((), ()))).astype(BF16)

    def row_sent(d):
        send("row", sem_x, d, x_hbm, xg.at[my_row]).wait_send()
        send("row", sem_w1, d, term.at[my_row], w1_in.at[my_row]).wait_send()
        send("row", sem_c, d, pc.at[my_row], pc_in.at[my_row]).wait_send()
        send("row", sem_w4, d, w4_in.at[my_row], w4_in.at[my_row]).wait_send()

    def col_sent(d):
        if scattered:
            send("col", sem_w2, d, small.at[pl.ds(0, piece)], w2_in.at[my_col]).wait_send()
            send("col", sem_w3, d, w3_in.at[my_col], w3_in.at[my_col]).wait_send()
        else:
            send("col", sem_w2, d, small, w2_in.at[my_col]).wait_send()

    def mate_sent(d):
        for p, some in enumerate(pieces):
            mine = up.at[my_col, some]
            gone = mate_part.at[0, some]
            move(sem_y, d * count_pieces + p, gone, mate_in.at[0, some], col=mate).wait_send()
            move(sem_f, d * count_pieces + p, mine, mine, col=mate).wait_send()

    def high_sent(d):
        for p, some in enumerate(pieces):
            mine = up.at[my_col, some]
            gone = part.at[0, some]
            index = (d - 1) * count_pieces + p
            move(sem_z, index, gone, part_in.at[0, some], col=mate).wait_send()
            move(sem_u, index, mine, mine, col=mate).wait_send()

    repeat(list(range(half)), mate_sent)
    repeat(list(range(1, half)), high_sent)
    repeat(col_steps, col_sent)

    def w4_wait(d):
        slot = w4_in.at[behind("row", d)]
        send("row", sem_w4, d, slot, slot).wait_recv()

    repeat(row_steps, w4_wait)
    wg_ref[...] = w4_in[...].reshape(width, width).astype(F32)
    repeat(row_steps, row_sent)


def finish(out_ref, ig_ref, wg_ref, out_hbm, ig_hbm, wg_hbm, sem):
    trio = ((out_ref, out_hbm), (ig_ref, ig_hbm), (wg_ref, wg_hbm))
    copies = [pltpu.make_async_copy(a, b, sem.at[i]) for i, (a, b) in enumerate(trio)]
    for copy in copies:
        copy.start()
    for copy in copies:
        copy.wait()


def body(node_features, layer_weight, output_grad, block_values, block_position, tile_count):
    rows, cols = lax.axis_size("row"), lax.axis_size("col")
    nodes, width = node_features.shape
    slots, block = block_values.shape[2], block_values.shape[3]
    assert nodes == block
    share = width // rows
    piece = share // cols
    if not (piece >= 8 and piece % 8 == 0):
        piece = share
    place = pl.BlockSpec(memory_space=pl.ANY)
    inside = pl.BlockSpec(memory_space=pltpu.VMEM)
    half = cols // 2
    assert cols == 2 * half
    dma = pltpu.SemaphoreType.DMA
    shapes = (
        jax.ShapeDtypeStruct((nodes, width), BF16),
        jax.ShapeDtypeStruct((nodes, width), BF16),
        jax.ShapeDtypeStruct((width, width), F32),
    )
    results = pl.pallas_call(
        functools.partial(kernel, rows, cols),
        out_shape=(
            pltpu.VMEM((nodes, width), BF16),
            pltpu.VMEM((nodes, width), BF16),
            pltpu.VMEM((width, width), F32),
        ),
        in_specs=[place, place, place, place, place, place],
        out_specs=(inside, inside, inside),
        scratch_shapes=[
            pltpu.SMEM((slots,), jnp.int32),
            pltpu.SMEM((1, 1), jnp.int32),
            pltpu.VMEM((slots + 1, block, block), BF16),
            pltpu.VMEM((width, width), BF16),
            pltpu.VMEM((nodes, width), BF16),
            pltpu.VMEM((rows, nodes, width), BF16),
            pltpu.VMEM((cols, nodes, rows * nodes), BF16),
            pltpu.VMEM((cols, rows * nodes, nodes), BF16),
            pltpu.VMEM((half, nodes, width), BF16),
            pltpu.VMEM((half, nodes, width), BF16),
            pltpu.VMEM((half, nodes, width), BF16),
            pltpu.VMEM((half, nodes, width), BF16),
            pltpu.VMEM((cols, nodes, width), BF16),
            pltpu.VMEM((rows * nodes, width), F32),
            pltpu.VMEM((rows, nodes, width), BF16),
            pltpu.VMEM((rows, nodes, width), BF16),
            pltpu.VMEM((rows, share, width), BF16),
            pltpu.VMEM((rows, share, width), BF16),
            pltpu.VMEM((nodes, width), F32),
            pltpu.VMEM((cols, piece, width), F32),
            pltpu.VMEM((share, width), F32),
            pltpu.VMEM((cols, piece, width), F32),
            pltpu.VMEM((rows, share, width), BF16),
            dma((7,)),
            dma((2, rows - 1)),
            dma((2, half * 2)),
            dma((2, (half - 1) * 2)),
            dma((2, (half - 1) * 2)),
            dma((2, half * 2)),
            dma((2, rows - 1)),
            dma((2, rows - 1)),
            dma((2, cols - 1)),
            dma((2, cols - 1)),
            dma((2, rows - 1)),
        ],
        compiler_params=pltpu.CompilerParams(collective_id=0, has_side_effects=True),
    )(
        block_position.reshape(slots),
        tile_count,
        node_features,
        layer_weight,
        output_grad,
        block_values.reshape(slots, block, block),
    )
    return pl.pallas_call(
        finish,
        out_shape=shapes,
        in_specs=[inside] * 3,
        out_specs=(place,) * 3,
        scratch_shapes=[
            dma((3,)),
        ],
        compiler_params=pltpu.CompilerParams(vmem_limit_bytes=4 << 20),
    )(*results)


def solution(mesh):
    in_specs = (
        P(("row", "col"), None),
        P(),
        P(("row", "col"), None),
        P("row", "col", None, None, None),
        P("row", "col", None),
        P("row", "col"),
    )
    out_specs = (P(("row", "col"), None), P(("row", "col"), None), P())
    return jax.shard_map(body, mesh=mesh, in_specs=in_specs, out_specs=out_specs, check_vma=False)
```
